32 devices in a mesh: dp: 2 (over y), context: 4 (over x, core), expert: 4 (over z).
Axes of the slice: x: 2, y: 2, z: 4, core: 2. Of those that a mesh axis runs over, the one named last changes fastest.
Arguments:
- prompt_rows: bfloat16 [4096, 768], P(('dp', 'context', 'expert')), may hold values from -6 to 6
- suffix_rows: bfloat16 [4, 8, 128, 768], P('context', ('dp', 'expert')), may hold values from -6 to 6
- prompt_cotangent: bfloat16 [4096, 768], P(('dp', 'context', 'expert')), may hold values from -6 to 6
- suffix_cotangent: bfloat16 [4, 8, 128, 768], P('context', ('dp', 'expert')), may hold values from -6 to 6
- project_weight: bfloat16 [768, 2304], P(('context', 'expert')), may hold values from -0.21875 to 0.21875
- output_weight: bfloat16 [768, 768], P(('context', 'expert')), may hold values from -0.625 to 0.625
- router_weight: bfloat16 [768, 16], P(('context', 'expert')), may hold values from -0.4375 to 0.4375
- first_gain: bfloat16 [768], P(('context', 'expert')), may hold values from 0.5 to 1.5
- second_gain: bfloat16 [768], P(('context', 'expert')), may hold values from 0.5 to 1.5
- bias_table: bfloat16 [32, 12], P(('context', 'expert')), may hold values from -4 to 4
- expert_up: bfloat16 [16, 768, 3072], P(('context', 'expert')), may hold values from -0.21875 to 0.21875
- expert_down: bfloat16 [16, 3072, 768], P(('context', 'expert')), may hold values from -0.109375 to 0.109375
- prompt_routes: int32 [4096, 2], P(('dp', 'context', 'expert')), may hold values from 0 to 15, all different within a row; in each aligned block of 128 rows (0 to 127, 128 to 255, ...) at most 32 rows name the same one
- suffix_routes: int32 [4, 8, 128, 2], P('context', ('dp', 'expert')), may hold values from 0 to 15, all different within a row; in each aligned block of 128 rows (0 to 127, 128 to 255, ..., all dimensions but the last counted through in order) at most 32 rows name the same one
- suffix_prompt: int32 [8], P(('dp', 'expert')), may hold values from 0 to 1
- bucket_index: int32 [1536], replicated, may hold values from 0 to 31, as said below
Outputs:
- prompt_out: bfloat16 [4096, 768], P(('dp', 'context', 'expert'))
- suffix_out: bfloat16 [4, 8, 128, 768], P('context', ('dp', 'expert'))
- prompt_grad: float32 [4096, 768], P(('dp', 'context', 'expert'))
- suffix_grad: float32 [4, 8, 128, 768], P('context', ('dp', 'expert'))
- project_grad: float32 [768, 2304], P(('context', 'expert'))
- output_grad: float32 [768, 768], P(('context', 'expert'))
- router_grad: float32 [768, 16], P(('context', 'expert'))
- first_gain_grad: float32 [768], P(('context', 'expert'))
- second_gain_grad: float32 [768], P(('context', 'expert'))
- table_grad: float32 [32, 12], P(('context', 'expert'))
- expert_up_grad: float32 [16, 768, 3072], P(('context', 'expert'), 'dp')
- expert_down_grad: float32 [16, 3072, 768], P(('context', 'expert'), 'dp')
The draws below stay inside these ranges and needn't reach their ends.
Inputs may be any that keep to these rules, and one draw needn't show every extreme that they name: `prompt_routes`: each row names 2 different experts. In the rows of one device (aligned blocks of 128 rows) no expert is named more than 32 times, and in every draw some block names some expert exactly 32 times. `suffix_routes`: each row names 2 different experts. In the rows of one device (aligned blocks of 128 rows, the first three dimensions taken in order) no expert is named more than 32 times, and in every draw some block names some expert exactly 32 times. Never falls as the distance grows; bucket_index[0] = 0 and bucket_index[1535] = 31.
All inputs are finite; a program needn't handle non-finite values.
Results may differ from the reference program's by a relative error of at most 0.02.
Values may be sent and summed in bfloat16 or wider, within the bound.
No kernel may reach another device: no remote copies, remote signals or barrier semaphores. Data moves between devices by JAX's collectives and lax.ppermute only.
A program may use at most 320 MiB of HBM per device.

```python
import math
import jax
import jax.numpy as jnp
import numpy as np
from jax import lax

D = 768
H = 12
HD = 64
FF = 3072
NB = 32
TOPK = 2
NPROMPT = 2
ROWS_DEV = 128
EXPERTS = 16
CAPH = 32
CAP = 64
PLEN = 1024
CLEN = 512
DIST = 1536
CONTS = 8
PTOK = 4096
N_DP = 2
N_CONTEXT = 4
N_EXPERT = 4


def draw_bucket_index(key, part):
    bound_count = NB - 2
    steps = jnp.arange(1, bound_count + 1, dtype=jnp.int32)
    centre = steps * steps * (DIST - 2) // ((NB - 1) * (NB - 1)) + steps
    jitter = jax.random.randint(key, (bound_count,), 0, 1 + bound_count, dtype=jnp.int32)
    bounds = jnp.minimum(jnp.sort(centre + jitter * steps // bound_count), DIST - 2)
    distance = jnp.arange(DIST, dtype=jnp.int32)
    bucket = jnp.sum((distance[:, None] >= bounds[None, :]).astype(jnp.int32), axis=1).astype(jnp.int32)
    return jnp.where(distance == DIST - 1, NB - 1, bucket).astype(jnp.int32)


def touch_ends(drawn, own_key, least, high):
    place = [jax.random.randint(jax.random.fold_in(own_key, axis), (), 0, length) for axis, length in enumerate(drawn.shape)]
    longest = drawn.shape.index(max(drawn.shape))
    next_to = place[:longest] + [(place[longest] + 1) % drawn.shape[longest]] + place[longest + 1:]
    return drawn.at[tuple(place)].set(least).at[tuple(next_to)].set(high)


def levels(stream_key, dims, cuts, least, high):
    factor_of, own = 1.0, jax.random.fold_in(stream_key, 6)
    for axis_at, shards_of in cuts:
        heights = jnp.exp(jax.random.uniform(jax.random.fold_in(own, axis_at), (shards_of,), jnp.float32, least / len(cuts), high / len(cuts)))
        factor_of = factor_of * jnp.repeat(heights, dims[axis_at] // shards_of).reshape([-1 if axis == axis_at else 1 for axis in range(len(dims))])
    return factor_of


def routed_block(rng, own, number, rows, number_of, top, bound, skew):
    order = jax.random.permutation(rng, number_of)
    packed, common = load_shares(number_of, rows * top, bound, skew, True), load_shares(number_of, rows * top, bound, skew, False)
    places = jnp.arange(number_of)

    def named(lengths, rotation):
        used = int((lengths > 0).sum())
        fixed = max(1, used // 4)
        shifted = fixed + (places - fixed + rotation * (used - fixed)) % max(1, number_of - fixed)
        return jnp.zeros((number_of,), jnp.int32).at[order[jnp.where(places < fixed, places, shifted)]].set(jnp.asarray(lengths, jnp.int32))

    lengths = jnp.where(number % 4 == 0, named(packed, number // 4), named(common, number - number // 4 - 1))
    mixed = jax.random.permutation(jax.random.fold_in(own, 3), number_of)
    giver, receiver = mixed[0:number_of // 2 * 2:2], mixed[1:number_of // 2 * 2:2]
    room = jnp.minimum(lengths[giver] - 1, bound - lengths[receiver]) // 2
    room = jnp.where((giver == order[0]) | (receiver == order[0]) | (lengths[receiver] == 0), 0, jnp.maximum(room, 0))
    shifted = jax.random.randint(jax.random.fold_in(own, 4), (number_of // 2,), 0, 1 << 20) % (room + 1)
    lengths = lengths.at[giver].add(-shifted).at[receiver].add(shifted)
    items = jnp.searchsorted(jnp.cumsum(lengths), jnp.arange(rows * top), side="right").astype(jnp.int32)
    grid = items.reshape(top, rows).T
    grid = grid[jax.random.permutation(jax.random.fold_in(own, 1), rows)]
    rotation = jax.random.randint(jax.random.fold_in(own, 2), (rows, 1), 0, top)
    return jnp.take_along_axis(grid, (jnp.arange(top)[None, :] + rotation) % top, axis=1)


def load_shares(count, total, reach, slope, full):
    weights = [(1 << 20) // math.isqrt(standing ** slope) + 1 for standing in range(1, count + 1)]
    largest = reach if full else min(reach, max(-(-total // count), total * weights[0] // sum(weights)))
    least = 1 if total - largest >= count - 1 else 0
    counts, spare = [largest] + [least] * (count - 1), total - largest - least * (count - 1)
    while spare > 0:
        movable = [i for i in range(1, count) if counts[i] < largest] or [i for i in range(1, count) if counts[i] < reach]
        pool, remaining = sum([weights[i] for i in movable]), spare
        for i in movable:
            addition = min(reach - counts[i], max(1, remaining * weights[i] // pool), spare)
            counts[i] = counts[i] + addition
            spare = spare - addition
    return np.array(counts)


def noise(own_key, dims, deviation, limit, pieces=(), kind=jnp.bfloat16):
    values = jax.random.normal(own_key, dims, jnp.float32) * deviation
    if len(pieces) > 0:
        values = levels(own_key, dims, pieces, -0.22, 0.18) * values
    return jnp.clip(values, min=-limit, max=limit).astype(kind)


def setup_inputs(seed: int = 0) -> dict:
    streams_of = jax.random.split(jax.random.key(seed), 17)
    prompt_rows = noise(streams_of[0], (PTOK, D), 1.0, 6.0, ((0, 32),))
    suffix_rows = noise(streams_of[1], (N_CONTEXT, CONTS, ROWS_DEV, D), 1.0, 6.0, ((0, 4), (1, 8)))
    prompt_cotangent = noise(streams_of[2], (PTOK, D), 1.0, 6.0, ((0, 32),))
    suffix_cotangent = noise(streams_of[3], (N_CONTEXT, CONTS, ROWS_DEV, D), 1.0, 6.0, ((0, 4), (1, 8)))
    project_weight = noise(streams_of[4], (D, 3 * D), D ** -0.5, 0.21875, ((0, 16),))
    output_weight = noise(streams_of[5], (D, D), (D // 8) ** -0.5, 0.625, ((0, 16),))
    router_weight = noise(streams_of[6], (D, EXPERTS), (D // 4) ** -0.5, 0.4375, ((0, 16),))
    first_gain = jnp.clip(1.0 + 0.1 * jax.random.normal(streams_of[7], (D,), jnp.float32), 0.5, 1.5).astype(jnp.bfloat16)
    second_gain = jnp.clip(1.0 + 0.1 * jax.random.normal(streams_of[8], (D,), jnp.float32), 0.5, 1.5).astype(jnp.bfloat16)
    bias_table = noise(streams_of[9], (NB, H), 1.0, 4.0, ((0, 16),))
    expert_up = noise(streams_of[10], (EXPERTS, D, FF), D ** -0.5, 0.21875, ((0, 16),))
    expert_down = noise(streams_of[11], (EXPERTS, FF, D), FF ** -0.5, 0.109375, ((0, 16),))
    prompt_routes_keys = jax.random.split(jax.random.fold_in(streams_of[12], 1), PTOK // ROWS_DEV)
    prompt_routes_turns = jax.random.permutation(jax.random.fold_in(streams_of[12], 3), PTOK // ROWS_DEV)
    prompt_routes = jax.vmap(lambda own, number: routed_block(jax.random.fold_in(streams_of[12], 2), own, number, ROWS_DEV, EXPERTS, TOPK, CAPH, 2))(prompt_routes_keys, prompt_routes_turns).reshape((PTOK, TOPK))
    suffix_routes_keys = jax.random.split(jax.random.fold_in(streams_of[13], 1), N_CONTEXT * CONTS * ROWS_DEV // ROWS_DEV)
    suffix_routes_turns = jax.random.permutation(jax.random.fold_in(streams_of[13], 3), N_CONTEXT * CONTS * ROWS_DEV // ROWS_DEV)
    suffix_routes = jax.vmap(lambda own, number: routed_block(jax.random.fold_in(streams_of[13], 2), own, number, ROWS_DEV, EXPERTS, TOPK, CAPH, 2))(suffix_routes_keys, suffix_routes_turns).reshape((N_CONTEXT, CONTS, ROWS_DEV, TOPK))
    suffix_prompt = touch_ends(jax.random.randint(streams_of[14], (CONTS,), 0, NPROMPT), jax.random.fold_in(streams_of[14], 1), 0, NPROMPT - 1).astype(jnp.int32)
    bucket_index = draw_bucket_index(jax.random.fold_in(streams_of[16], 71), 0)
    return dict(prompt_rows=prompt_rows, suffix_rows=suffix_rows, prompt_cotangent=prompt_cotangent, suffix_cotangent=suffix_cotangent, project_weight=project_weight, output_weight=output_weight, router_weight=router_weight, first_gain=first_gain, second_gain=second_gain, bias_table=bias_table, expert_up=expert_up, expert_down=expert_down, prompt_routes=prompt_routes, suffix_routes=suffix_routes, suffix_prompt=suffix_prompt, bucket_index=bucket_index)


EPS = 1e-06
NEGATIVE = -1e+30
HIGHEST = lax.Precision.HIGHEST

@jax.custom_vjp
def low(v):
    return lax.optimization_barrier(v.astype(jnp.bfloat16)).astype(jnp.float32)

@jax.custom_vjp
def low_back(v):
    return v

def low_keep(v):
    return (low(v), None)

def low_pass(kept, grad):
    return (grad,)

def back_keep(v):
    return (v, None)

def back_low(kept, grad):
    return (low(grad),)
low.defvjp(low_keep, low_pass)
low_back.defvjp(back_keep, back_low)

def norm_apply(rows_in, gain):
    return rows_in * lax.rsqrt(lax.optimization_barrier(jnp.mean(rows_in * rows_in, axis=-1, keepdims=True)) + EPS) * gain

def gelu_tanh(values_in):
    inner_term = 0.7978845608028654 * (values_in + 0.044715 * values_in * values_in * values_in)
    return 0.5 * values_in * (1.0 + jnp.tanh(inner_term))

def gate_values(logits, routes):
    probabilities = jax.nn.softmax(logits, axis=-1)
    onehot = (routes[:, :, None] == jnp.arange(logits.shape[-1], dtype=jnp.int32)[None, None, :]).astype(jnp.float32)
    chosen = lax.optimization_barrier(jnp.sum(probabilities[:, None, :] * onehot, axis=-1))
    return chosen / lax.optimization_barrier(jnp.sum(chosen, axis=-1, keepdims=True))

def slot_rank(routes, experts):
    flat_routes = routes.reshape(-1)
    onehot = (flat_routes[:, None] == jnp.arange(experts, dtype=jnp.int32)[None, :]).astype(jnp.int32)
    before = jnp.cumsum(onehot, axis=0).astype(jnp.int32) - onehot
    return lax.optimization_barrier(jnp.sum(before * onehot, axis=1)).astype(jnp.int32).reshape(routes.shape)

def attention(queries, key_rows, value_rows, bias_rows, query_pos, key_pos):
    query_count = queries.shape[0]
    key_count = key_rows.shape[0]
    query_heads = queries.reshape(query_count, H, HD)
    key_heads = key_rows.reshape(key_count, H, HD)
    value_heads = value_rows.reshape(key_count, H, HD)
    distance = query_pos[:, None] - key_pos[None, :]
    bias_values = jnp.take(bias_rows, jnp.clip(distance, 0, DIST - 1), axis=1)
    raw_scores = jnp.einsum('qhd,khd->hqk', query_heads, key_heads, precision=HIGHEST) / math.sqrt(HD)
    scores = low_back(raw_scores + bias_values)
    scores = jnp.where(distance[None] >= 0, scores, NEGATIVE)
    probabilities = low(jax.nn.softmax(scores, axis=-1))
    mixture = jnp.einsum('hqk,khd->qhd', probabilities, value_heads, precision=HIGHEST)
    return low(low_back(mixture.reshape(query_count, D)))

def one_group(weights, items):
    project, output, router, gain_first, gain_second, bias_rows, up_weight, down_weight = weights
    prompt_in, suffix_in, prompt_routes_g, suffix_routes_g, chosen_prompts = items
    group_size = N_CONTEXT * N_EXPERT
    half_rows = group_size * ROWS_DEV
    inputs = jnp.concatenate([prompt_in, suffix_in.reshape(half_rows, D)], axis=0)
    normed = low(norm_apply(inputs, gain_first))
    projected = low(low_back(jnp.dot(normed, project, precision=HIGHEST)))
    prompt_part = projected[:half_rows].reshape(NPROMPT, PLEN, 3 * D)
    suffix_part = projected[half_rows:].reshape(N_CONTEXT, N_EXPERT, ROWS_DEV, 3 * D).transpose(1, 0, 2, 3).reshape(N_EXPERT, CLEN, 3 * D)
    prompt_pos = jnp.arange(PLEN, dtype=jnp.int32)

    def prompt_attend(sequence):
        return attention(sequence[:, :D], sequence[:, D:2 * D], sequence[:, 2 * D:], bias_rows, prompt_pos, prompt_pos)
    prompt_mix = lax.map(jax.checkpoint(prompt_attend), prompt_part)
    query_pos = PLEN + jnp.arange(CLEN, dtype=jnp.int32)
    key_pos = jnp.arange(PLEN + CLEN, dtype=jnp.int32)

    def suffix_attend(pair_items):
        sequence, chosen = pair_items
        earlier = lax.dynamic_index_in_dim(prompt_part, chosen, 0, keepdims=False)
        key_rows = jnp.concatenate([earlier[:, D:2 * D], sequence[:, D:2 * D]], axis=0)
        value_rows = jnp.concatenate([earlier[:, 2 * D:], sequence[:, 2 * D:]], axis=0)
        return attention(sequence[:, :D], key_rows, value_rows, bias_rows, query_pos, key_pos)
    suffix_mix = lax.map(jax.checkpoint(suffix_attend), (suffix_part, chosen_prompts))
    mixture = jnp.concatenate([prompt_mix.reshape(half_rows, D), suffix_mix.reshape(N_EXPERT, N_CONTEXT, ROWS_DEV, D).transpose(1, 0, 2, 3).reshape(half_rows, D)], axis=0)
    hidden = inputs + low_back(jnp.dot(mixture, output, precision=HIGHEST))
    moe_in = low(norm_apply(hidden, gain_second))
    logits = jnp.dot(moe_in, router, precision=HIGHEST)
    routes = jnp.concatenate([prompt_routes_g.reshape(half_rows, TOPK), suffix_routes_g.reshape(half_rows, TOPK)], axis=0)
    gate_weights = gate_values(logits, routes)
    source = jnp.arange(group_size, dtype=jnp.int32)[:, None, None] * CAP
    prompt_slots = prompt_routes_g * (group_size * CAP) + source + jax.vmap(lambda block: slot_rank(block, EXPERTS))(prompt_routes_g)
    suffix_slots = suffix_routes_g * (group_size * CAP) + source + CAPH + jax.vmap(lambda block: slot_rank(block, EXPERTS))(suffix_routes_g)
    slot_index = jnp.concatenate([prompt_slots.reshape(half_rows, TOPK), suffix_slots.reshape(half_rows, TOPK)], axis=0).astype(jnp.int32)
    buffer_rows = EXPERTS * group_size * CAP
    dispatch = jnp.zeros((buffer_rows, D), jnp.float32).at[slot_index.reshape(-1)].set(jnp.repeat(moe_in, TOPK, axis=0))
    up_sums = low_back(jnp.einsum('esd,edf->esf', dispatch.reshape(EXPERTS, group_size * CAP, D), up_weight, precision=HIGHEST))
    activation = low(gelu_tanh(up_sums))
    produced = low(low_back(jnp.einsum('esf,efd->esd', activation, down_weight, precision=HIGHEST))).reshape(buffer_rows, D)
    picked = produced[slot_index]
    result = hidden + lax.optimization_barrier(jnp.sum(gate_weights[:, :, None] * picked, axis=1))
    return (result[:half_rows], result[half_rows:].reshape(N_CONTEXT, N_EXPERT, ROWS_DEV, D))

def reference(prompt_rows, suffix_rows, prompt_cotangent, suffix_cotangent, project_weight, output_weight, router_weight, first_gain, second_gain, bias_table, expert_up, expert_down, prompt_routes, suffix_routes, suffix_prompt, bucket_index):
    group_size = N_CONTEXT * N_EXPERT
    bucket_hot = (bucket_index[:, None] == jnp.arange(NB, dtype=jnp.int32)[None, :]).astype(jnp.float32)
    prompt_groups = prompt_routes.reshape(N_DP, group_size, ROWS_DEV, TOPK)
    suffix_groups = suffix_routes.reshape(N_CONTEXT, N_DP, N_EXPERT, ROWS_DEV, TOPK).transpose(1, 0, 2, 3, 4).reshape(N_DP, group_size, ROWS_DEV, TOPK)
    chosen_all = suffix_prompt.reshape(N_DP, N_EXPERT)

    def forward(prompt_in, suffix_in, project, output, router, gain_first, gain_second, table_full, up_weight, down_weight):
        bias_rows = jnp.dot(bucket_hot, table_full, precision=HIGHEST).T
        weights = (project, output, router, gain_first, gain_second, bias_rows, up_weight, down_weight)
        prompt_split = prompt_in.reshape(N_DP, group_size * ROWS_DEV, D)
        suffix_split = suffix_in.reshape(N_CONTEXT, N_DP, N_EXPERT, ROWS_DEV, D).transpose(1, 0, 2, 3, 4)
        checked = jax.checkpoint(one_group)
        prompt_result, suffix_result = lax.map(lambda items: checked(weights, items), (prompt_split, suffix_split, prompt_groups, suffix_groups, chosen_all))
        return (prompt_result.reshape(PTOK, D), suffix_result.transpose(1, 0, 2, 3, 4).reshape(N_CONTEXT, CONTS, ROWS_DEV, D))
    primals = tuple((array_in.astype(jnp.float32) for array_in in (prompt_rows, suffix_rows, project_weight, output_weight, router_weight, first_gain, second_gain, bias_table, expert_up, expert_down)))
    results, pullback = jax.vjp(forward, *primals)
    grads = pullback((prompt_cotangent.astype(jnp.float32), suffix_cotangent.astype(jnp.float32)))
    return (results[0].astype(jnp.bfloat16), results[1].astype(jnp.bfloat16), grads[0], grads[1], grads[2], grads[3], grads[4], grads[5], grads[6], grads[7], grads[8], grads[9])
```

```python
import functools

import jax
import jax.numpy as jnp
from jax import lax
from jax.experimental import pallas as pl
from jax.experimental.pallas import tpu as pltpu
from jax.sharding import PartitionSpec as P

NPROMPT = 2
EPS = 1e-06
NEGATIVE = -1e30
HIGHEST = lax.Precision.HIGHEST
BF = jnp.bfloat16
F32 = jnp.float32


def dot(a, b, lhs=1, rhs=0):
    return lax.dot_general(a, b, (((lhs,), (rhs,)), ((), ())), preferred_element_type=F32)


def context_bits():
    size, bits = lax.axis_size("context"), []
    while size > 1:
        size //= 2
        bits.append(size)
    return bits


def context_swap(x, bit):
    n = lax.axis_size("context")
    return lax.ppermute(x, "context", [(i, i ^ bit) for i in range(n)])


def shift(x, axis, k):
    n = lax.axis_size(axis)
    return lax.ppermute(x, axis, [(i, (i + k) % n) for i in range(n)])


def gather_context(pieces):
    for bit in context_bits():
        for key in list(pieces):
            pieces[(key[0] ^ bit,) + key[1:]] = context_swap(pieces[key], bit)
    return pieces


def gather_group(x):
    nz = lax.axis_size("expert")
    pieces = {(0, 0): x}
    for k in range(1, nz):
        pieces[(0, k)] = shift(x, "expert", k)
    return gather_context(pieces)


def group_order():
    nc, nz = lax.axis_size("context"), lax.axis_size("expert")
    c, z = lax.axis_index("context"), lax.axis_index("expert")
    ck = jnp.arange(nc, dtype=jnp.int32)[:, None]
    zk = jnp.arange(nz, dtype=jnp.int32)[None, :]
    source = (c ^ ck) * nz + (z + nz - zk) % nz
    target = (c ^ ck) * nz + (z + zk) % nz
    return source.reshape(-1), target.reshape(-1)


def reduce_context(v):
    for bit in reversed(context_bits()):
        n = v.shape[0] // 2
        keep = v.reshape(n, 2, *v.shape[1:])
        v = (keep[:, 0].astype(F32) + context_swap(keep[:, 1], bit).astype(F32)).astype(BF)
    return v[0]


def reduce_expert(v):
    total = v[0].astype(F32)
    for k in range(1, v.shape[0]):
        total = total + shift(v[k], "expert", k).astype(F32)
    return total


def reduce_group(v):
    width = v.shape[-1]
    cut = width * 2 // 3 // 128 * 128
    bits = list(reversed(context_bits()))
    n = v.shape[0] // 2
    pair = v.reshape(n, 2, *v.shape[1:])
    v = (pair[:, 0].astype(F32) + context_swap(pair[:, 1], bits[0]).astype(F32)).astype(BF)
    first, second = v[..., :cut], v[..., cut:]
    second = jnp.stack([reduce_expert(second[i]).astype(BF) for i in range(n)])
    for bit in bits[1:]:
        n //= 2
        first = first.reshape(n, 2, *first.shape[1:])
        first = (first[:, 0].astype(F32) + context_swap(first[:, 1], bit).astype(F32)).astype(BF)
        second = second.reshape(n, 2, *second.shape[1:])
        second = (second[:, 0].astype(F32) + context_swap(second[:, 1], bit).astype(F32)).astype(BF)
    first = reduce_expert(first[0])
    return jnp.concatenate([first, second[0].astype(F32)], axis=-1)


def reduce_dp(x):
    low = x.astype(BF)
    total = low.astype(F32)
    for k in range(1, lax.axis_size("dp")):
        total = total + shift(low, "dp", k).astype(F32)
    return total


def across(buffer):
    return lax.all_to_all(buffer, ("context", "expert"), split_axis=0, concat_axis=0, tiled=True)


def project_kernel(dims, meta, gain_ref, *refs):
    group, nc, rows, width, prompt_rows = dims
    x_in, s_in, w_in = refs[:group], refs[group : group + nc], refs[group + nc : 2 * group + nc]
    q_ref, kv_ref, normed_ref, w_ref, x_scr, sems = refs[2 * group + nc :]
    step = pl.program_id(0)
    wrows = width // group
    qtiles = width // 256

    @pl.when(step == 0)
    def _():
        copies = []
        for k in range(group):
            at = pl.multiple_of(meta[k] * rows, rows)
            copies.append(pltpu.make_async_copy(x_in[k], x_scr.at[pl.ds(at, rows), :], sems.at[len(copies)]))
        for k in range(nc):
            at = pl.multiple_of(prompt_rows + meta[group + k] * rows, rows)
            copies.append(pltpu.make_async_copy(s_in[k], x_scr.at[pl.ds(at, rows), :], sems.at[len(copies)]))
        for k in range(group):
            at = pl.multiple_of(meta[k] * wrows, 8)
            copies.append(pltpu.make_async_copy(w_in[k], w_ref.at[pl.ds(at, wrows), :], sems.at[len(copies)]))
        for c in copies:
            c.start()
        for c in copies:
            c.wait()
        total = x_scr.shape[0]
        gain = gain_ref[...]

        def norm(i, carry):
            at = pl.ds(pl.multiple_of(i * rows, rows), rows)
            x = x_scr[at, :].astype(F32)
            scale = lax.rsqrt(jnp.mean(x * x, axis=-1, keepdims=True) + EPS)
            normed_ref[at, :] = (x * scale * gain).astype(BF)
            return carry

        lax.fori_loop(0, total // rows, norm, 0)

    at = pl.ds(pl.multiple_of(step * 256, 256), 256)

    @pl.when(step < qtiles)
    def _():
        own = pl.ds(pl.multiple_of(meta[group + nc] * rows, rows), rows)
        own_s = pl.ds(pl.multiple_of(prompt_rows + meta[group + nc + 1] * rows, rows), rows)
        w = w_ref[:, at]
        q_ref[:rows, :] = dot(normed_ref[own, :], w).astype(BF)
        q_ref[rows:, :] = dot(normed_ref[own_s, :], w).astype(BF)

    @pl.when(step >= qtiles)
    def _():
        kv_ref[...] = dot(normed_ref[...], w_ref[:, at]).astype(BF)


def project(meta, gain, x_pieces, s_pieces, w_pieces, group, nc):
    rows, width = x_pieces[0].shape
    prompt_rows = group * rows
    total = prompt_rows + nc * rows
    wcols = w_pieces[0].shape[1]
    qt = width // 256
    any_spec = pl.BlockSpec(memory_space=pl.ANY)
    n = 2 * group + nc
    return pl.pallas_call(
        functools.partial(project_kernel, (group, nc, rows, width, prompt_rows)),
        grid_spec=pltpu.PrefetchScalarGridSpec(
            num_scalar_prefetch=1,
            grid=(3 * qt,),
            in_specs=[pl.BlockSpec((1, width), lambda i, m: (0, 0))] + [any_spec] * n,
            out_specs=[
                pl.BlockSpec((2 * rows, 256), lambda i, m: (0, jnp.minimum(i, qt - 1))),
                pl.BlockSpec((total, 256), lambda i, m: (0, jnp.maximum(i - qt, 0))),
                pl.BlockSpec((total, width), lambda i, m: (0, 0)),
                pl.BlockSpec((width, wcols), lambda i, m: (0, 0)),
            ],
            scratch_shapes=[pltpu.VMEM((total, width), BF), pltpu.SemaphoreType.DMA((n,))],
        ),
        out_shape=[
            jax.ShapeDtypeStruct((2 * rows, width), BF),
            jax.ShapeDtypeStruct((total, 2 * width), BF),
            jax.ShapeDtypeStruct((total, width), BF),
            jax.ShapeDtypeStruct((width, wcols), BF),
        ],
        compiler_params=pltpu.CompilerParams(dimension_semantics=("arbitrary",), vmem_limit_bytes=60 << 20),
        cost_estimate=pl.CostEstimate(flops=2 * total * width * 2 * width, bytes_accessed=20 << 20, transcendentals=0),
        name="project",
    )(meta, gain, *x_pieces, *s_pieces, *w_pieces)


def half_masks(rows):
    lane = lax.broadcasted_iota(jnp.int32, (rows, 128), 1)
    return lane < 64


def stack_halves(x):
    low = half_masks(x.shape[0])
    zero = jnp.zeros_like(x)
    return jnp.concatenate([jnp.where(low, x, zero), jnp.where(low, zero, x)], axis=0)


def pick_halves(y):
    n = y.shape[0] // 2
    return jnp.where(half_masks(n), y[:n], y[n:])


def bias_of(table, bucket):
    nb = table.shape[1]
    hot = (lax.broadcasted_iota(jnp.int32, (nb, bucket.shape[1]), 0) == bucket).astype(BF)
    return jnp.where(bucket < 0, NEGATIVE, dot(table, hot))


def toeplitz(row, rows, count):
    width = row.shape[1]
    tall = jnp.broadcast_to(row, (rows, width))
    return pltpu.roll(tall, width - rows, 1, stride=1, stride_axis=0)[:, :count]


def attend_kernel(meta, q_ref, ko, kc, ks, vo, vc, vs, table, bp, bs, mix_ref, pp_ref, ps_ref, wp, ws):
    step = pl.program_id(0)
    rows = q_ref.shape[0] // 2

    @pl.when(step == 0)
    def _():
        wp[...] = bias_of(table[...], bp[...])
        ws[...] = bias_of(table[...], bs[...])

    def soft(scores):
        top = jnp.max(scores, axis=-1, keepdims=True)
        e = jnp.exp(scores - top)
        return e * (1.0 / jnp.sum(e, axis=-1, keepdims=True))

    def biases(w, count):
        return jnp.concatenate(
            [toeplitz(w[pl.ds(2 * step + i, 1), :], rows, count) for i in range(2)], axis=0
        )

    q = stack_halves(q_ref[:rows, :])
    scores = dot(q, ko[...], 1, 1) * 0.125 + biases(wp, ko.shape[0])
    p = soft(scores).astype(BF)
    pp_ref[0] = p
    mix_ref[:rows, :] = pick_halves(dot(p, vo[...])).astype(BF)

    q = stack_halves(q_ref[rows:, :])
    far = kc.shape[0]
    keys = jnp.concatenate([kc[...], ks[...]], axis=0)
    scores = dot(q, keys, 1, 1) * 0.125 + biases(ws, far + ks.shape[0])
    p = soft(scores).astype(BF)
    ps_ref[0] = p
    mix = dot(p[:, :far], vc[...]) + dot(p[:, far:], vs[...])
    mix_ref[rows:, :] = pick_halves(mix).astype(BF)


def key_specs(plen, slen, width):
    tiles = width // 128

    def at(kind, base):
        if kind == "own":
            return pl.BlockSpec((plen, 128), lambda h, m: (m[0], base + h))
        if kind == "far":
            return pl.BlockSpec((plen, 128), lambda h, m: (m[1], base + h))
        return pl.BlockSpec((slen, 128), lambda h, m: (m[2], base + h))

    return [at(kind, base) for base in (0, tiles) for kind in ("own", "far", "near")]


def attend(meta, q, kv, table, bp, bs, plen, slen):
    rows2, width = q.shape
    rows = rows2 // 2
    pairs = width // 128
    const = lambda h, m: (0, 0)
    return pl.pallas_call(
        attend_kernel,
        grid_spec=pltpu.PrefetchScalarGridSpec(
            num_scalar_prefetch=1,
            grid=(pairs,),
            in_specs=[pl.BlockSpec((rows2, 128), lambda h, m: (0, h))]
            + key_specs(plen, slen, width)
            + [pl.BlockSpec(t.shape, const) for t in (table, bp, bs)],
            out_specs=[
                pl.BlockSpec((rows2, 128), lambda h, m: (0, h)),
                pl.BlockSpec((1, rows2, plen), lambda h, m: (h, 0, 0)),
                pl.BlockSpec((1, rows2, plen + slen), lambda h, m: (h, 0, 0)),
            ],
            scratch_shapes=[
                pltpu.VMEM((table.shape[0], bp.shape[1]), F32),
                pltpu.VMEM((table.shape[0], bs.shape[1]), F32),
            ],
        ),
        out_shape=[
            jax.ShapeDtypeStruct((rows2, width), BF),
            jax.ShapeDtypeStruct((pairs, rows2, plen), BF),
            jax.ShapeDtypeStruct((pairs, rows2, plen + slen), BF),
        ],
        compiler_params=pltpu.CompilerParams(dimension_semantics=("arbitrary",), vmem_limit_bytes=60 << 20),
        cost_estimate=pl.CostEstimate(
            flops=8 * rows * (2 * plen + slen) * width, bytes_accessed=16 << 20, transcendentals=0
        ),
        name="attend",
    )(meta, q, kv, kv, kv, kv, kv, kv, table, bp, bs)


def attend_back_kernel(meta, q_ref, g_ref, ko, kc, ks, vo, vc, vs, pp_ref, ps_ref, dq_ref, dk_ref, dv_ref, sp_ref, ss_ref):
    step = pl.program_id(0)
    rows = q_ref.shape[0] // 2
    plen, slen = ko.shape[0], ks.shape[0]
    back = lax.broadcasted_iota(jnp.int32, (rows, rows), 0) + lax.broadcasted_iota(jnp.int32, (rows, rows), 1)
    flip = (back == rows - 1).astype(BF)

    @pl.when(step == 0)
    def _():
        sp_ref[...] = jnp.zeros_like(sp_ref)
        ss_ref[...] = jnp.zeros_like(ss_ref)

    def grads(p_low, dp):
        p = p_low.astype(F32)
        centre = jnp.sum(p * dp, axis=-1, keepdims=True)
        return (p * (dp - centre)).astype(BF)

    def diagonals(ds, out):
        width = out.shape[1]
        for i in range(2):
            turned = dot(flip, ds[i * rows : (i + 1) * rows])
            wide = jnp.concatenate([turned, jnp.zeros((rows, width - turned.shape[1]), F32)], axis=1)
            moved = pltpu.roll(wide, 1, 1, stride=1, stride_axis=0)
            out[pl.ds(2 * step + i, 1), :] = jnp.sum(moved, axis=0, keepdims=True)

    q = stack_halves(q_ref[:rows, :])
    g = stack_halves(g_ref[:rows, :])
    p = pp_ref[0]
    ds = grads(p, dot(g, vo[...], 1, 1))
    dq_ref[:rows, :] = (pick_halves(dot(ds, ko[...])) * 0.125).astype(BF)
    dk_own = dot(ds, q, 0, 0) * 0.125
    dv_own = dot(p, g, 0, 0)
    diagonals(ds, sp_ref)
    own = pl.ds(pl.multiple_of(meta[0] * plen, plen), plen)
    other = pl.ds(pl.multiple_of((1 - meta[0]) * plen, plen), plen)
    dk_ref[own, :] = dk_own.astype(BF)
    dv_ref[own, :] = dv_own.astype(BF)
    dk_ref[other, :] = jnp.zeros((plen, 128), BF)
    dv_ref[other, :] = jnp.zeros((plen, 128), BF)

    q = stack_halves(q_ref[rows:, :])
    g = stack_halves(g_ref[rows:, :])
    p = ps_ref[0]
    values = jnp.concatenate([vc[...], vs[...]], axis=0)
    ds = grads(p, dot(g, values, 1, 1))
    dq = dot(ds[:, :plen], kc[...]) + dot(ds[:, plen:], ks[...])
    dq_ref[rows:, :] = (pick_halves(dq) * 0.125).astype(BF)
    diagonals(ds, ss_ref)
    far = pl.ds(pl.multiple_of(meta[1] * plen, plen), plen)
    near = pl.ds(2 * plen, slen)
    dk = dot(ds, q, 0, 0) * 0.125
    dv = dot(p, g, 0, 0)
    dk_ref[far, :] = (dk_ref[far, :].astype(F32) + dk[:plen]).astype(BF)
    dv_ref[far, :] = (dv_ref[far, :].astype(F32) + dv[:plen]).astype(BF)
    dk_ref[near, :] = dk[plen:].astype(BF)
    dv_ref[near, :] = dv[plen:].astype(BF)


def attend_back(meta, q, g, kv, pp, ps, bp, bs, plen, slen):
    rows2, width = q.shape
    rows = rows2 // 2
    pairs = width // 128
    total = kv.shape[0]
    heads = 16
    const = lambda h, m: (0, 0)
    column = lambda h, m: (0, h)
    return pl.pallas_call(
        attend_back_kernel,
        grid_spec=pltpu.PrefetchScalarGridSpec(
            num_scalar_prefetch=1,
            grid=(pairs,),
            in_specs=[pl.BlockSpec((rows2, 128), column)] * 2
            + key_specs(plen, slen, width)
            + [
                pl.BlockSpec((1, rows2, plen), lambda h, m: (h, 0, 0)),
                pl.BlockSpec((1, rows2, plen + slen), lambda h, m: (h, 0, 0)),
            ],
            out_specs=[
                pl.BlockSpec((rows2, 128), column),
                pl.BlockSpec((total, 128), column),
                pl.BlockSpec((total, 128), column),
                pl.BlockSpec((heads, bp.shape[1]), const),
                pl.BlockSpec((heads, bs.shape[1]), const),
            ],
        ),
        out_shape=[
            jax.ShapeDtypeStruct((rows2, width), BF),
            jax.ShapeDtypeStruct((total, width), BF),
            jax.ShapeDtypeStruct((total, width), BF),
            jax.ShapeDtypeStruct((heads, bp.shape[1]), F32),
            jax.ShapeDtypeStruct((heads, bs.shape[1]), F32),
        ],
        compiler_params=pltpu.CompilerParams(dimension_semantics=("arbitrary",), vmem_limit_bytes=60 << 20),
        cost_estimate=pl.CostEstimate(
            flops=20 * rows * (2 * plen + slen) * width, bytes_accessed=30 << 20, transcendentals=0
        ),
        name="attend_back",
    )(meta, q, g, kv, kv, kv, kv, kv, kv, pp, ps)


def expert_kernel(a_ref, c_ref, up_ref, down_ref, act_ref, u_ref, back_ref, acc, gg):
    step = pl.program_id(0)
    width = acc.shape[1]

    @pl.when(step == 0)
    def _():
        acc[...] = jnp.zeros_like(acc)
        gg[...] = jnp.zeros_like(gg)

    rows = acc.shape[0]
    block = 256

    def part(i, carry):
        at = pl.ds(pl.multiple_of(i * block, block), block)
        v = dot(a_ref[at, :width], up_ref[0])
        h = dot(c_ref[at, :], down_ref[0], 1, 1)
        square = v * v
        t = jnp.tanh(v * (0.7978845608028654 + 0.7978845608028654 * 0.044715 * square))
        half = 0.5 * (1.0 + t)
        act = v * half
        slope = half + 0.5 * v * (1.0 - t * t) * (0.7978845608028654 + 3 * 0.7978845608028654 * 0.044715 * square)
        low = act.astype(BF)
        act_ref[at, :] = low
        u = (h * slope).astype(BF)
        u_ref[at, :] = u
        gg[at, :] += jnp.broadcast_to(jnp.sum(low.astype(F32) * h, axis=1, keepdims=True), (block, 128))
        acc[at, :] += dot(u, up_ref[0], 1, 1)
        return carry

    lax.fori_loop(0, rows // block, part, 0)

    @pl.when(step == pl.num_programs(0) - 1)
    def _():
        back_ref[:, :width] = acc[...].astype(BF)
        g = gg[...]
        high = g.astype(BF)
        low = (g - high.astype(F32)).astype(BF)
        lane = lax.broadcasted_iota(jnp.int32, g.shape, 1)
        back_ref[:, width:] = jnp.where(lane == 0, high, jnp.where(lane == 1, low, jnp.zeros_like(low)))


def expert_pass(arrived, cot, up, down):
    rows = arrived.shape[0]
    width, hidden = up.shape[1:]
    tile = 512
    const = lambda j: (0, 0)
    return pl.pallas_call(
        expert_kernel,
        grid=(hidden // tile,),
        in_specs=[
            pl.BlockSpec(arrived.shape, const),
            pl.BlockSpec(cot.shape, const),
            pl.BlockSpec((1, width, tile), lambda j: (0, 0, j)),
            pl.BlockSpec((1, tile, width), lambda j: (0, j, 0)),
        ],
        out_specs=[
            pl.BlockSpec((rows, tile), lambda j: (0, j)),
            pl.BlockSpec((rows, tile), lambda j: (0, j)),
            pl.BlockSpec((rows, width + 128), const),
        ],
        scratch_shapes=[pltpu.VMEM((rows, width), F32), pltpu.VMEM((rows, 128), F32)],
        out_shape=[
            jax.ShapeDtypeStruct((rows, hidden), BF),
            jax.ShapeDtypeStruct((rows, hidden), BF),
            jax.ShapeDtypeStruct((rows, width + 128), BF),
        ],
        compiler_params=pltpu.CompilerParams(dimension_semantics=("arbitrary",), vmem_limit_bytes=60 << 20),
        cost_estimate=pl.CostEstimate(flops=6 * rows * width * hidden, bytes_accessed=30 << 20, transcendentals=0),
        name="experts",
    )(arrived, cot, up, down)


def slots_of(routes, experts, capacity, base):
    hot = [(routes[:, s : s + 1] == jnp.arange(experts, dtype=jnp.int32)[None, :]) for s in range(2)]
    count = (hot[0] | hot[1]).astype(BF)
    n = routes.shape[0]
    before = jnp.arange(n, dtype=jnp.int32)
    tri = (before[:, None] > before[None, :]).astype(BF)
    rank = dot(tri, count)
    return jnp.stack([jnp.sum(jnp.where(h, rank, 0.0), axis=1) for h in hot], axis=1).astype(jnp.int32) + (
        routes * capacity + base
    )


def norm_back(x, gain, dy):
    scale = lax.rsqrt(jnp.mean(x * x, axis=-1, keepdims=True) + EPS)
    hat = x * scale
    gy = dy * gain
    dx = scale * (gy - hat * jnp.mean(gy * hat, axis=-1, keepdims=True))
    return dx, jnp.sum(dy * hat, axis=0)


def body(
    prompt_rows,
    suffix_rows,
    prompt_cotangent,
    suffix_cotangent,
    project_weight,
    output_weight,
    router_weight,
    first_gain,
    second_gain,
    bias_table,
    expert_up,
    expert_down,
    prompt_routes,
    suffix_routes,
    suffix_prompt,
    bucket_index,
):
    rows, width = prompt_rows.shape
    heads = bias_table.shape[1]
    experts = router_weight.shape[1]
    topk = prompt_routes.shape[1]
    nc, nz, ndp = (lax.axis_size(a) for a in ("context", "expert", "dp"))
    group = nc * nz
    c, z, d = (lax.axis_index(a) for a in ("context", "expert", "dp"))
    owner = c * nz + z
    plen = rows * group // NPROMPT
    slen = rows * nc
    half_capacity = 2 * topk * rows // experts
    capacity = 2 * half_capacity
    slots = experts * capacity
    wrows = width // group
    tbrows = bias_table.shape[0]

    source, target = group_order()
    source_c = c ^ jnp.arange(nc, dtype=jnp.int32)

    suffix_route_rows = suffix_routes.reshape(rows, topk)
    routes = jnp.concatenate([prompt_routes, suffix_route_rows], axis=0)
    flat_slots = jnp.concatenate(
        [
            slots_of(prompt_routes, experts, capacity, 0),
            slots_of(suffix_route_rows, experts, capacity, half_capacity),
        ],
        axis=0,
    )
    slot_ids = jnp.arange(slots, dtype=jnp.int32)[None, :]
    hots = [(flat_slots[:, s : s + 1] == slot_ids).astype(BF) for s in range(topk)]
    cot_low = jnp.concatenate([prompt_cotangent, suffix_cotangent.reshape(rows, width)], axis=0)
    cot_sent = dot(hots[0] + hots[1], cot_low, 0, 0).astype(BF)

    extra = jnp.concatenate(
        [
            router_weight,
            first_gain[:, None],
            second_gain[:, None],
            jnp.pad(bias_table, ((0, wrows - bias_table.shape[0]), (0, 0))),
        ],
        axis=1,
    )
    lanes = 128
    extra = jnp.pad(extra, ((0, 0), (0, lanes - extra.shape[1])))
    w_pieces = gather_group(project_weight)
    x_pieces = gather_group(prompt_rows)
    s_pieces = gather_context({(0,): suffix_rows.reshape(rows, width)})
    o_pieces = gather_group(jnp.concatenate([output_weight, extra], axis=1))
    keys = [(i, j) for i in range(nc) for j in range(nz)]
    back_order = jnp.argsort(source)
    o_full = jnp.take(jnp.stack([o_pieces[k] for k in keys]), back_order, axis=0).reshape(width, -1)
    output_full = o_full[:, :width]
    extras = o_full[:, width:]
    router_full = extras[:, :experts]
    gain_one = extras[:, experts].astype(F32)
    gain_two = extras[:, experts + 1].astype(F32)
    table_full = extras.reshape(group, wrows, lanes)[:, : tbrows, experts + 2 : experts + 2 + heads]
    table_full = table_full.reshape(-1, heads)
    nb = table_full.shape[0]
    table16 = jnp.pad(table_full.T, ((0, 16 - heads), (0, 0)))

    meta = jnp.concatenate([source, source_c, owner[None], c[None]]).astype(jnp.int32)
    q, kv, normed, project_full = project(
        meta,
        gain_one[None, :],
        [x_pieces[k] for k in keys],
        [s_pieces[(i,)] for i in range(nc)],
        [w_pieces[k] for k in keys],
        group,
        nc,
    )

    cot_arrived = across(cot_sent.reshape(group, capacity, width)).reshape(slots, width)

    own_prompt = owner * rows // plen
    first_p = owner * rows - own_prompt * plen
    first_s = plen + c * rows
    dist = bucket_index.shape[0]
    ladder = jnp.concatenate(
        [
            jnp.zeros((rows,), jnp.int32),
            jnp.flip(bucket_index),
            jnp.full((max(plen, slen) + rows,), -1, jnp.int32),
        ]
    )
    bp = lax.dynamic_slice_in_dim(ladder, dist - 1 - first_p, plen + rows)[None, :]
    bs = lax.dynamic_slice_in_dim(ladder, dist - 1 - first_s, plen + slen + rows)[None, :]
    places = jnp.stack([own_prompt, suffix_prompt[0], jnp.int32(NPROMPT * plen // slen)]).astype(jnp.int32)
    mixture, pp, ps = attend(places, q, kv, table16, bp, bs, plen, slen)

    inputs = jnp.concatenate([prompt_rows, suffix_rows.reshape(rows, width)], axis=0).astype(F32)
    hidden = inputs + dot(mixture, output_full)
    scale_two = lax.rsqrt(jnp.mean(hidden * hidden, axis=-1, keepdims=True) + EPS)
    moe_in = (hidden * scale_two * gain_two).astype(BF)
    logits = dot(moe_in, router_full)
    eids = jnp.arange(experts, dtype=jnp.int32)[None, :]
    route_hot = [(routes[:, s : s + 1] == eids) for s in range(topk)]
    chosen = [jnp.sum(jnp.where(h, logits, 0.0), axis=1, keepdims=True) for h in route_hot]
    gates = [jax.nn.sigmoid(chosen[0] - chosen[1]), jax.nn.sigmoid(chosen[1] - chosen[0])]

    lane = jnp.arange(lanes, dtype=jnp.int32)[None, :]

    def lanes_of(g):
        high = g.astype(BF)
        low = (g - high.astype(F32)).astype(BF)
        return jnp.where(lane == 0, high, jnp.where(lane == 1, low, jnp.zeros_like(low)))

    both_hot = jnp.concatenate(hots, axis=0)
    sent = jnp.concatenate(
        [jnp.concatenate([moe_in, lanes_of(g)], axis=1) for g in gates], axis=0
    )
    dispatch = dot(both_hot, sent, 0, 0).astype(BF)
    arrived = across(dispatch.reshape(group, capacity, width + lanes)).reshape(slots, width + lanes)

    act, u, back = expert_pass(arrived, cot_arrived, expert_up, expert_down)
    back_in = across(back.reshape(group, capacity, width + lanes)).reshape(slots, width + lanes)
    gate_in = jnp.sum(arrived[:, width:].astype(F32), axis=1, keepdims=True)
    tokens = arrived[:, :width]
    gated_cot = (gate_in * cot_arrived.astype(F32)).astype(BF)
    gated_u = (gate_in * u.astype(F32)).astype(BF)

    def exchanged(make):
        total = None
        for k in range(1, ndp):
            got = shift(make((d + k) % ndp).astype(BF), "dp", k).astype(F32)
            total = got if total is None else total + got
        mine = make(d)
        return mine if total is None else mine + total

    hidden_units = expert_up.shape[2]
    down_rows, up_rows = hidden_units // ndp, width // ndp
    down_shard = exchanged(
        lambda i: dot(lax.dynamic_slice_in_dim(act, i * down_rows, down_rows, 1), gated_cot, 0, 0)
    )
    up_shard = exchanged(
        lambda i: dot(lax.dynamic_slice_in_dim(tokens, i * up_rows, up_rows, 1), gated_u, 0, 0)
    )
    produced = dot(act, expert_down[0]).astype(BF)

    picks = [dot(h, back_in) for h in hots]
    gate_grad = [p[:, width] + p[:, width + 1] for p in picks]
    spread = (gates[0] * gates[1]) * (gate_grad[0] - gate_grad[1])[:, None]
    logit_grad = jnp.where(route_hot[0], spread, 0.0) - jnp.where(route_hot[1], spread, 0.0)
    moe_grad = (
        gates[0] * picks[0][:, :width]
        + gates[1] * picks[1][:, :width]
        + lax.dot_general(logit_grad, router_full.astype(F32), (((1,), (1,)), ((), ())), precision=HIGHEST)
    )
    router_grad = dot(moe_in, logit_grad.astype(BF), 0, 0)
    cot = cot_low.astype(F32)
    hidden_grad, second_grad = norm_back(hidden, gain_two, moe_grad)
    hidden_grad = hidden_grad + cot
    branch_grad = hidden_grad.astype(BF)
    output_grad = dot(mixture, branch_grad, 0, 0)
    mixture_grad = dot(branch_grad, output_full, 1, 1).astype(BF)

    returned = across(produced.reshape(group, capacity, width)).reshape(slots, width)
    result = hidden + gates[0] * dot(hots[0], returned) + gates[1] * dot(hots[1], returned)

    dq, dk, dv, sum_p, sum_s = attend_back(places, q, mixture_grad, kv, pp, ps, bp, bs, plen, slen)
    hot_p = (bp.T == jnp.arange(nb, dtype=jnp.int32)[None, :]).astype(F32)
    hot_s = (bs.T == jnp.arange(nb, dtype=jnp.int32)[None, :]).astype(F32)
    table_grad = (jnp.dot(sum_p, hot_p, precision=HIGHEST) + jnp.dot(sum_s, hot_s, precision=HIGHEST))[:heads].T

    wq, wk, wv = (project_full[:, i * width : (i + 1) * width] for i in range(3))
    normed_grad = (dot(dk, wk, 1, 1) + dot(dv, wv, 1, 1)).astype(BF)
    prompt_part = jnp.take(normed_grad[: group * rows].reshape(group, rows, width), target, axis=0)
    prompt_part = reduce_group(prompt_part.reshape(nc, nz, rows, width))
    suffix_part = reduce_context(jnp.take(normed_grad[group * rows :].reshape(nc, rows, width), source_c, axis=0))
    own_normed = jnp.concatenate(
        [
            lax.dynamic_slice_in_dim(normed, owner * rows, rows, 0),
            lax.dynamic_slice_in_dim(normed, group * rows + c * rows, rows, 0),
        ],
        axis=0,
    )
    project_grad = jnp.concatenate(
        [dot(own_normed, dq, 0, 0), dot(normed, dk, 0, 0), dot(normed, dv, 0, 0)], axis=1
    ).astype(BF)
    table_block = jnp.pad(
        table_grad.reshape(group, tbrows, heads), ((0, 0), (0, wrows - tbrows), (0, lanes - heads))
    ).astype(BF)
    side = jnp.pad(
        jnp.concatenate([router_grad, second_grad[:, None]], axis=1), ((0, 0), (0, lanes - experts - 1))
    ).astype(BF)

    def relative(a):
        return jnp.take(a.reshape(group, wrows, -1), target, axis=0).reshape(nc, nz, wrows, -1)

    early = reduce_dp(reduce_group(relative(jnp.concatenate([output_grad.astype(BF), side], axis=1))))
    late = reduce_dp(
        reduce_group(relative(jnp.concatenate([project_grad, table_block.reshape(width, lanes)], axis=1)))
    )
    project_shard = late[:, : 3 * width]
    first_shard = jnp.sum(project_shard * project_weight.astype(F32), axis=1) / first_gain.astype(F32)

    normed_total = jnp.concatenate([prompt_part, suffix_part.astype(F32)], axis=0) + dot(dq, wq, 1, 1)
    input_grad, _ = norm_back(inputs, gain_one, normed_total)
    input_grad = input_grad + hidden_grad
    return (
        result[:rows].astype(BF),
        result[rows:].astype(BF).reshape(suffix_rows.shape),
        input_grad[:rows],
        input_grad[rows:].reshape(suffix_rows.shape),
        project_shard,
        early[:, :width],
        early[:, width : width + experts],
        first_shard,
        early[:, width + experts],
        late[:tbrows, 3 * width : 3 * width + heads],
        up_shard[None],
        down_shard[None],
    )


def solution(mesh):
    return jax.shard_map(
        body,
        mesh=mesh,
        in_specs=(
            P(("dp", "context", "expert"), None),
            P("context", ("dp", "expert"), None, None),
            P(("dp", "context", "expert"), None),
            P("context", ("dp", "expert"), None, None),
            P(("context", "expert"), None),
            P(("context", "expert"), None),
            P(("context", "expert"), None),
            P(("context", "expert")),
            P(("context", "expert")),
            P(("context", "expert"), None),
            P(("context", "expert"), None, None),
            P(("context", "expert"), None, None),
            P(("dp", "context", "expert"), None),
            P("context", ("dp", "expert"), None, None),
            P(("dp", "expert")),
            P(),
        ),
        out_specs=(
            P(("dp", "context", "expert"), None),
            P("context", ("dp", "expert"), None, None),
            P(("dp", "context", "expert"), None),
            P("context", ("dp", "expert"), None, None),
            P(("context", "expert"), None),
            P(("context", "expert"), None),
            P(("context", "expert"), None),
            P(("context", "expert")),
            P(("context", "expert")),
            P(("context", "expert"), None),
            P(("context", "expert"), "dp", None),
            P(("context", "expert"), "dp", None),
        ),
        check_vma=False,
    )
```

```python
import functools

import jax
import jax.numpy as jnp
from jax import lax
from jax.experimental import pallas as pl
from jax.experimental.pallas import tpu as pltpu
from jax.sharding import PartitionSpec as P


NPROMPT = 2
EPS = 1e-06
NEGATIVE = -1e30
HIGHEST = lax.Precision.HIGHEST
BF = jnp.bfloat16
F32 = jnp.float32

PARAMS = pltpu.CompilerParams(dimension_semantics=("arbitrary",), vmem_limit_bytes=60 << 20)


def dot(a, b, lhs=1, rhs=0):
    return lax.dot_general(a, b, (((lhs,), (rhs,)), ((), ())), preferred_element_type=F32)


def context_bits():
    size, bits = lax.axis_size("context"), []
    while size > 1:
        size //= 2
        bits.append(size)
    return bits


def context_swap(x, bit):
    n = lax.axis_size("context")
    return lax.ppermute(x, "context", [(i, i ^ bit) for i in range(n)])


def shift(x, axis, k):
    n = lax.axis_size(axis)
    return lax.ppermute(x, axis, [(i, (i + k) % n) for i in range(n)])


def gather_context(pieces):
    for bit in context_bits():
        for key in list(pieces):
            pieces[(key[0] ^ bit,) + key[1:]] = context_swap(pieces[key], bit)
    return pieces


def gather_group(x):
    nz = lax.axis_size("expert")
    pieces = {(0, 0): x}
    for k in range(1, nz):
        pieces[(0, k)] = shift(x, "expert", k)
    return gather_context(pieces)


def add_low(*terms):
    return sum(t.astype(F32) for t in terms).astype(BF)


def reduce_expert(v):
    total = v[0].astype(F32)
    for k in range(1, v.shape[0]):
        total = total + shift(v[k], "expert", k).astype(F32)
    return total


def reduce_rows(keep0, keep1, send0, send1, nz):
    x_bit, core_bit = context_bits()
    got1 = context_swap(send1, core_bit)
    got0 = context_swap(send0, core_bit)
    got = context_swap(add_low(keep1, got1), x_bit)
    total = keep0.astype(F32) + got0.astype(F32) + got.astype(F32)
    return reduce_expert(total[:nz].astype(BF)), total[nz:]


def reduce_dp(x):
    low = x.astype(BF)
    total = low.astype(F32)
    for k in range(1, lax.axis_size("dp")):
        total = total + shift(low, "dp", k).astype(F32)
    return total


def across(buffer):
    return lax.all_to_all(buffer, ("context", "expert"), split_axis=0, concat_axis=0, tiled=True)


def project_kernel(dims, meta, *refs):
    group, nc, rows, width, prompt_rows, experts = dims
    p_in, s_in = refs[:group], refs[group : group + nc]
    q_ref, kv_ref, normed_ref, w_ref, extras_ref, gains_ref, x_scr, sems = refs[group + nc :]
    step = pl.program_id(0)
    wrows = width // group
    qtiles = width // 256

    @pl.when(step == 0)
    def _():
        copies = []

        def copy(src, dst):
            copies.append(pltpu.make_async_copy(src, dst, sems.at[len(copies)]))

        for k in range(group):
            for i in range(wrows // 8):
                at = pl.multiple_of(meta[k] * wrows + 8 * i, 8)
                copy(
                    p_in[k].at[rows + 3 * wrows :, i * 128 : (i + 1) * 128],
                    extras_ref.at[pl.ds(at, 8), :],
                )
        first = len(copies)
        for k in range(group):
            at = pl.multiple_of(meta[k] * rows, rows)
            copy(p_in[k].at[:rows, :], x_scr.at[pl.ds(at, rows), :])
        for k in range(nc):
            at = pl.multiple_of(prompt_rows + meta[group + k] * rows, rows)
            copy(s_in[k], x_scr.at[pl.ds(at, rows), :])
        second = len(copies)
        for k in range(group):
            at = pl.multiple_of(meta[k] * wrows, 8)
            for i in range(3):
                copy(
                    p_in[k].at[rows + i * wrows : rows + (i + 1) * wrows, :],
                    w_ref.at[pl.ds(at, wrows), i * width : (i + 1) * width],
                )
        for c in copies:
            c.start()
        for c in copies[:first]:
            c.wait()
        extras = extras_ref[...]
        pick = lax.broadcasted_iota(jnp.int32, (8, extras.shape[1]), 1)
        pick = (pick == experts + lax.broadcasted_iota(jnp.int32, pick.shape, 0)).astype(BF)
        gains = dot(pick, extras, 1, 1)
        gains_ref[...] = gains
        gain = gains[0:1, :]
        for c in copies[first:second]:
            c.wait()

        def norm(i, carry):
            at = pl.ds(pl.multiple_of(i * rows, rows), rows)
            x = x_scr[at, :].astype(F32)
            scale = lax.rsqrt(jnp.mean(x * x, axis=-1, keepdims=True) + EPS)
            normed_ref[at, :] = (x * scale * gain).astype(BF)
            return carry

        lax.fori_loop(0, x_scr.shape[0] // rows, norm, 0)
        for c in copies[second:]:
            c.wait()

    at = pl.ds(pl.multiple_of(step * 256, 256), 256)

    @pl.when(step < qtiles)
    def _():
        own = pl.ds(pl.multiple_of(meta[group + nc] * rows, rows), rows)
        own_s = pl.ds(pl.multiple_of(prompt_rows + meta[group + nc + 1] * rows, rows), rows)
        mine = jnp.concatenate([normed_ref[own, :], normed_ref[own_s, :]], axis=0)
        q_ref[...] = dot(mine, w_ref[:, at]).astype(BF)

    @pl.when(step >= qtiles)
    def _():
        kv_ref[...] = dot(normed_ref[...], w_ref[:, at]).astype(BF)


def project(meta, pieces, s_pieces, group, nc, experts):
    rows, width = s_pieces[0].shape
    prompt_rows = group * rows
    total = prompt_rows + nc * rows
    wcols = 3 * width
    qt = width // 256
    any_spec = pl.BlockSpec(memory_space=pl.ANY)
    n = group + nc
    copies = group * (4 + width // group // 8) + nc
    return pl.pallas_call(
        functools.partial(project_kernel, (group, nc, rows, width, prompt_rows, experts)),
        grid_spec=pltpu.PrefetchScalarGridSpec(
            num_scalar_prefetch=1,
            grid=(3 * qt,),
            in_specs=[any_spec] * n,
            out_specs=[
                pl.BlockSpec((2 * rows, 256), lambda i, m: (0, jnp.minimum(i, qt - 1))),
                pl.BlockSpec((total, 256), lambda i, m: (0, jnp.maximum(i - qt, 0))),
                pl.BlockSpec((total, width), lambda i, m: (0, 0)),
                pl.BlockSpec((width, wcols), lambda i, m: (0, 0)),
                pl.BlockSpec((width, 128), lambda i, m: (0, 0)),
                pl.BlockSpec((8, width), lambda i, m: (0, 0)),
            ],
            scratch_shapes=[pltpu.VMEM((total, width), BF), pltpu.SemaphoreType.DMA((copies,))],
        ),
        out_shape=[
            jax.ShapeDtypeStruct((2 * rows, width), BF),
            jax.ShapeDtypeStruct((total, 2 * width), BF),
            jax.ShapeDtypeStruct((total, width), BF),
            jax.ShapeDtypeStruct((width, wcols), BF),
            jax.ShapeDtypeStruct((width, 128), BF),
            jax.ShapeDtypeStruct((8, width), F32),
        ],
        compiler_params=PARAMS,
        cost_estimate=pl.CostEstimate(flops=2 * total * width * 2 * width, bytes_accessed=20 << 20, transcendentals=0),
        name="project",
    )(meta, *pieces, *s_pieces)


def half_masks(rows):
    lane = lax.broadcasted_iota(jnp.int32, (rows, 128), 1)
    return lane < 64


def stack_halves(x):
    low = half_masks(x.shape[0])
    zero = jnp.zeros_like(x)
    return jnp.concatenate([jnp.where(low, x, zero), jnp.where(low, zero, x)], axis=0)


def pick_halves(y):
    n = y.shape[0] // 2
    return jnp.where(half_masks(n), y[:n], y[n:])


def bucket_hot(nb, bucket, dtype):
    return (lax.broadcasted_iota(jnp.int32, (nb, bucket.shape[1]), 0) == bucket).astype(dtype)


def bias_of(table, bucket):
    return jnp.where(bucket < 0, NEGATIVE, dot(table, bucket_hot(table.shape[1], bucket, BF)))


def table_of(dims, extras):
    experts, nb, tbrows, wrows = dims
    spot = lax.broadcasted_iota(jnp.int32, (nb, extras.shape[0]), 0)
    spot = spot // tbrows * wrows + spot % tbrows
    pick = (lax.broadcasted_iota(jnp.int32, spot.shape, 1) == spot).astype(BF)
    found = dot(pick, extras).astype(BF)
    lane = lax.broadcasted_iota(jnp.int32, (16, extras.shape[1]), 1)
    head = (lane == experts + 2 + lax.broadcasted_iota(jnp.int32, lane.shape, 0)).astype(BF)
    return dot(head, found, 1, 1).astype(BF)


def toeplitz(row, rows, count):
    width = row.shape[1]
    tall = jnp.broadcast_to(row, (rows, width))
    return pltpu.roll(tall, width - rows, 1, stride=1, stride_axis=0)[:, :count]


def attend_kernel(dims, meta, q_ref, ko, kc, ks, vo, vc, vs, extras, bp, bs, mix_ref, pp_ref, ps_ref, wp, ws):
    step = pl.program_id(0)
    rows = q_ref.shape[0] // 2

    @pl.when(step == 0)
    def _():
        table = table_of(dims, extras[...])
        wp[...] = bias_of(table, bp[...])
        ws[...] = bias_of(table, bs[...])

    def soft(scores):
        top = jnp.max(scores, axis=-1, keepdims=True)
        e = jnp.exp(scores - top)
        return e * (1.0 / jnp.sum(e, axis=-1, keepdims=True))

    def biases(w, count):
        return jnp.concatenate(
            [toeplitz(w[pl.ds(2 * step + i, 1), :], rows, count) for i in range(2)], axis=0
        )

    q = stack_halves(q_ref[:rows, :])
    scores = dot(q, ko[...], 1, 1) * 0.125 + biases(wp, ko.shape[0])
    p = soft(scores).astype(BF)
    pp_ref[0] = p
    mix_ref[:rows, :] = pick_halves(dot(p, vo[...])).astype(BF)

    q = stack_halves(q_ref[rows:, :])
    far = kc.shape[0]
    keys = jnp.concatenate([kc[...], ks[...]], axis=0)
    scores = dot(q, keys, 1, 1) * 0.125 + biases(ws, far + ks.shape[0])
    p = soft(scores).astype(BF)
    ps_ref[0] = p
    mix = dot(p[:, :far], vc[...]) + dot(p[:, far:], vs[...])
    mix_ref[rows:, :] = pick_halves(mix).astype(BF)


def key_specs(plen, slen, width):
    tiles = width // 128

    def at(kind, base):
        if kind == "own":
            return pl.BlockSpec((plen, 128), lambda h, m: (m[0], base + h))
        if kind == "far":
            return pl.BlockSpec((plen, 128), lambda h, m: (m[1], base + h))
        return pl.BlockSpec((slen, 128), lambda h, m: (m[2], base + h))

    return [at(kind, base) for base in (0, tiles) for kind in ("own", "far", "near")]


def attend(dims, meta, q, kv, extras, bp, bs, plen, slen):
    rows2, width = q.shape
    rows = rows2 // 2
    pairs = width // 128
    const = lambda h, m: (0, 0)
    return pl.pallas_call(
        functools.partial(attend_kernel, dims),
        grid_spec=pltpu.PrefetchScalarGridSpec(
            num_scalar_prefetch=1,
            grid=(pairs,),
            in_specs=[pl.BlockSpec((rows2, 128), lambda h, m: (0, h))]
            + key_specs(plen, slen, width)
            + [pl.BlockSpec(t.shape, const) for t in (extras, bp, bs)],
            out_specs=[
                pl.BlockSpec((rows2, 128), lambda h, m: (0, h)),
                pl.BlockSpec((1, rows2, plen), lambda h, m: (h, 0, 0)),
                pl.BlockSpec((1, rows2, plen + slen), lambda h, m: (h, 0, 0)),
            ],
            scratch_shapes=[
                pltpu.VMEM((16, bp.shape[1]), F32),
                pltpu.VMEM((16, bs.shape[1]), F32),
            ],
        ),
        out_shape=[
            jax.ShapeDtypeStruct((rows2, width), BF),
            jax.ShapeDtypeStruct((pairs, rows2, plen), BF),
            jax.ShapeDtypeStruct((pairs, rows2, plen + slen), BF),
        ],
        compiler_params=PARAMS,
        cost_estimate=pl.CostEstimate(
            flops=8 * rows * (2 * plen + slen) * width, bytes_accessed=16 << 20, transcendentals=0
        ),
        name="attend",
    )(meta, q, kv, kv, kv, kv, kv, kv, extras, bp, bs)


def attend_back_kernel(
    meta, q_ref, g_ref, ko, kc, ks, vo, vc, vs, pp_ref, ps_ref, bp, bs, dq_ref, dk_ref, dv_ref, table_ref, sp_ref, ss_ref
):
    step = pl.program_id(0)
    rows = q_ref.shape[0] // 2
    plen, slen = ko.shape[0], ks.shape[0]
    back = lax.broadcasted_iota(jnp.int32, (rows, rows), 0) + lax.broadcasted_iota(jnp.int32, (rows, rows), 1)
    flip = (back == rows - 1).astype(BF)

    @pl.when(step == 0)
    def _():
        sp_ref[...] = jnp.zeros_like(sp_ref)
        ss_ref[...] = jnp.zeros_like(ss_ref)

    def grads(p_low, dp):
        p = p_low.astype(F32)
        centre = jnp.sum(p * dp, axis=-1, keepdims=True)
        return (p * (dp - centre)).astype(BF)

    def diagonals(ds, out):
        width = out.shape[1]
        for i in range(2):
            turned = dot(flip, ds[i * rows : (i + 1) * rows])
            wide = jnp.concatenate([turned, jnp.zeros((rows, width - turned.shape[1]), F32)], axis=1)
            moved = pltpu.roll(wide, 1, 1, stride=1, stride_axis=0)
            out[pl.ds(2 * step + i, 1), :] = jnp.sum(moved, axis=0, keepdims=True)

    q = stack_halves(q_ref[:rows, :])
    g = stack_halves(g_ref[:rows, :])
    p = pp_ref[0]
    ds = grads(p, dot(g, vo[...], 1, 1))
    dq_ref[:rows, :] = (pick_halves(dot(ds, ko[...])) * 0.125).astype(BF)
    dk_own = dot(ds, q, 0, 0) * 0.125
    dv_own = dot(p, g, 0, 0)
    diagonals(ds, sp_ref)
    own = pl.ds(pl.multiple_of(meta[0] * plen, plen), plen)
    other = pl.ds(pl.multiple_of((1 - meta[0]) * plen, plen), plen)
    dk_ref[own, :] = dk_own.astype(BF)
    dv_ref[own, :] = dv_own.astype(BF)
    dk_ref[other, :] = jnp.zeros((plen, 128), BF)
    dv_ref[other, :] = jnp.zeros((plen, 128), BF)

    q = stack_halves(q_ref[rows:, :])
    g = stack_halves(g_ref[rows:, :])
    p = ps_ref[0]
    values = jnp.concatenate([vc[...], vs[...]], axis=0)
    ds = grads(p, dot(g, values, 1, 1))
    dq = dot(ds[:, :plen], kc[...]) + dot(ds[:, plen:], ks[...])
    dq_ref[rows:, :] = (pick_halves(dq) * 0.125).astype(BF)
    diagonals(ds, ss_ref)
    far = pl.ds(pl.multiple_of(meta[1] * plen, plen), plen)
    near = pl.ds(2 * plen, slen)
    dk = dot(ds, q, 0, 0) * 0.125
    dv = dot(p, g, 0, 0)
    dk_ref[far, :] = (dk_ref[far, :].astype(F32) + dk[:plen]).astype(BF)
    dv_ref[far, :] = (dv_ref[far, :].astype(F32) + dv[:plen]).astype(BF)
    dk_ref[near, :] = dk[plen:].astype(BF)
    dv_ref[near, :] = dv[plen:].astype(BF)

    @pl.when(step == pl.num_programs(0) - 1)
    def _():
        nb = table_ref.shape[0]
        sums = [
            lax.dot_general(
                bucket_hot(nb, b[...], F32), s[...], (((1,), (1,)), ((), ())), precision=HIGHEST, preferred_element_type=F32
            )
            for b, s in ((bp, sp_ref), (bs, ss_ref))
        ]
        table_ref[...] = sums[0] + sums[1]


def attend_back(meta, q, g, kv, pp, ps, bp, bs, plen, slen, nb):
    rows2, width = q.shape
    rows = rows2 // 2
    pairs = width // 128
    total = kv.shape[0]
    heads = 16
    const = lambda h, m: (0, 0)
    column = lambda h, m: (0, h)
    return pl.pallas_call(
        attend_back_kernel,
        grid_spec=pltpu.PrefetchScalarGridSpec(
            num_scalar_prefetch=1,
            grid=(pairs,),
            in_specs=[pl.BlockSpec((rows2, 128), column)] * 2
            + key_specs(plen, slen, width)
            + [
                pl.BlockSpec((1, rows2, plen), lambda h, m: (h, 0, 0)),
                pl.BlockSpec((1, rows2, plen + slen), lambda h, m: (h, 0, 0)),
                pl.BlockSpec(bp.shape, const),
                pl.BlockSpec(bs.shape, const),
            ],
            out_specs=[
                pl.BlockSpec((rows2, 128), column),
                pl.BlockSpec((total, 128), column),
                pl.BlockSpec((total, 128), column),
                pl.BlockSpec((nb, heads), const),
            ],
            scratch_shapes=[pltpu.VMEM((heads, bp.shape[1]), F32), pltpu.VMEM((heads, bs.shape[1]), F32)],
        ),
        out_shape=[
            jax.ShapeDtypeStruct((rows2, width), BF),
            jax.ShapeDtypeStruct((total, width), BF),
            jax.ShapeDtypeStruct((total, width), BF),
            jax.ShapeDtypeStruct((nb, heads), F32),
        ],
        compiler_params=PARAMS,
        cost_estimate=pl.CostEstimate(
            flops=20 * rows * (2 * plen + slen) * width, bytes_accessed=30 << 20, transcendentals=0
        ),
        name="attend_back",
    )(meta, q, g, kv, kv, kv, kv, kv, kv, pp, ps, bp, bs)


def one_hot_columns(column, count):
    return (lax.broadcasted_iota(jnp.int32, (column.shape[0], count), 1) == column).astype(BF)


def lane_pair(g, first):
    high = g.astype(BF)
    low = (g - high.astype(F32)).astype(BF)
    lane = lax.broadcasted_iota(jnp.int32, (g.shape[0], 128), 1)
    zero = jnp.zeros((g.shape[0], 128), BF)
    return jnp.where(lane == first, high, jnp.where(lane == first + 1, low, zero))


def post_kernel(dims, meta, x_ref, s_ref, mix_ref, extras, gains, cols, slot_rows, *refs):
    group, _ = dims
    o_in = refs[:group]
    hidden_ref, moe_ref, gates_ref, sent_ref, wo_ref, sems = refs[group:]
    width = x_ref.shape[1]
    wrows = width // group
    copies = []
    for k in range(group):
        at = pl.multiple_of(meta[k] * wrows, 8)
        copies.append(pltpu.make_async_copy(o_in[k], wo_ref.at[pl.ds(at, wrows), :], sems.at[k]))
    for c in copies:
        c.start()
    for c in copies:
        c.wait()
    rows = x_ref.shape[0]
    mixed = dot(mix_ref[...], wo_ref[...])
    hidden_ref[:rows, :] = x_ref[...].astype(F32) + mixed[:rows]
    hidden_ref[rows:, :] = s_ref[...].astype(F32) + mixed[rows:]
    hidden = hidden_ref[...]
    scale = lax.rsqrt(jnp.mean(hidden * hidden, axis=-1, keepdims=True) + EPS)
    moe_in = (hidden * scale * gains[1:2, :]).astype(BF)
    moe_ref[...] = moe_in
    logits = dot(moe_in, extras[...])
    lane = lax.broadcasted_iota(jnp.int32, logits.shape, 1)
    chosen = [
        jnp.sum(jnp.where(lane == cols[:, 2 + i : 3 + i], logits, 0.0), axis=1, keepdims=True) for i in range(2)
    ]
    gates = [1.0 / (1.0 + jnp.exp(chosen[1 - i] - chosen[i])) for i in range(2)]
    gates_ref[...] = jnp.where(lane == 0, gates[0], jnp.where(lane == 1, gates[1], 0.0))
    slots = sent_ref.shape[0]
    spot = lax.broadcasted_iota(jnp.int32, (slots, 2 * rows), 0)
    hot = [(spot == slot_rows[i : i + 1, :]).astype(BF) for i in range(2)]
    sent_ref[:, :width] = dot(hot[0] + hot[1], moe_in).astype(BF)
    sent_ref[:, width:] = (dot(hot[0], lane_pair(gates[0], 0)) + dot(hot[1], lane_pair(gates[1], 0))).astype(BF)


def post(meta, x, s, mixture, extras, gains, cols, slot_rows, o_pieces, group, experts, slots):
    rows, width = x.shape
    full = lambda a: pl.BlockSpec(a.shape, lambda i, m: (0,) * a.ndim)
    outs = [
        jax.ShapeDtypeStruct((2 * rows, width), F32),
        jax.ShapeDtypeStruct((2 * rows, width), BF),
        jax.ShapeDtypeStruct((2 * rows, 128), F32),
        jax.ShapeDtypeStruct((slots, width + 128), BF),
        jax.ShapeDtypeStruct((width, width), BF),
    ]
    return pl.pallas_call(
        functools.partial(post_kernel, (group, experts)),
        grid_spec=pltpu.PrefetchScalarGridSpec(
            num_scalar_prefetch=1,
            grid=(1,),
            in_specs=[full(a) for a in (x, s, mixture, extras, gains, cols, slot_rows)]
            + [pl.BlockSpec(memory_space=pl.ANY)] * group,
            out_specs=[full(o) for o in outs],
            scratch_shapes=[pltpu.SemaphoreType.DMA((group,))],
        ),
        out_shape=outs,
        compiler_params=PARAMS,
        cost_estimate=pl.CostEstimate(flops=2 << 30, bytes_accessed=6 << 20, transcendentals=0),
        name="post",
    )(meta, x, s, mixture, extras, gains, cols, slot_rows, *o_pieces)


def combine_kernel(
    dims, meta, back_ref, hidden_ref, moe_ref, gates_ref, mix_ref, wo_ref, extras, gains, cols, pc_ref, sc_ref,
    grad_ref, mixg_ref, keep0, keep1, send0, send1, scr,
):
    nz, experts = dims
    width = hidden_ref.shape[1]
    rows = pc_ref.shape[0]
    slots = back_ref.shape[0]
    gates = gates_ref[...]
    gate = [gates[:, i : i + 1] for i in range(2)]
    picks = [dot(one_hot_columns(cols[:, i : i + 1], slots), back_ref[...]) for i in range(2)]
    gate_grad = [p[:, width : width + 1] + p[:, width + 1 : width + 2] for p in picks]
    spread = gate[0] * gate[1] * (gate_grad[0] - gate_grad[1])
    lane = lax.broadcasted_iota(jnp.int32, gates.shape, 1)
    zero = jnp.zeros_like(gates)
    logit_grad = jnp.where(lane == cols[:, 2:3], spread, zero) - jnp.where(lane == cols[:, 3:4], spread, zero)
    high = logit_grad.astype(BF)
    low = (logit_grad - high.astype(F32)).astype(BF)
    moe_grad = gate[0] * picks[0][:, :width] + gate[1] * picks[1][:, :width]
    moe_grad = moe_grad + dot(high, extras[...], 1, 1) + dot(low, extras[...], 1, 1)
    hidden = hidden_ref[...]
    scale = lax.rsqrt(jnp.mean(hidden * hidden, axis=-1, keepdims=True) + EPS)
    hat = hidden * scale
    gy = moe_grad * gains[1:2, :]
    grad = scale * (gy - hat * jnp.mean(gy * hat, axis=-1, keepdims=True))
    grad_ref[:rows, :] = grad[:rows] + pc_ref[...].astype(F32)
    grad_ref[rows:, :] = grad[rows:] + sc_ref[...].astype(F32)
    branch = grad_ref[...].astype(BF)
    mixg_ref[...] = dot(branch, wo_ref[...], 1, 1).astype(BF)
    scr[:, :width] = dot(mix_ref[...], branch, 0, 0)
    mark = (lane == experts).astype(BF)
    scr[:, width:] = dot(moe_ref[...], high, 0, 0) + dot((moe_grad * hat).astype(BF), mark, 0, 0)
    wrows = width // (4 * nz)
    n = 0
    for out in (keep0, keep1, send0, send1):
        for k in range(nz):
            out[k] = scr[pl.ds(pl.multiple_of(meta[n] * wrows, 8), wrows), :].astype(BF)
            n += 1


def combine(meta, back, hidden, moe_in, gates, mixture, wo, extras, gains, cols, pc, sc, nz, experts):
    rows, width = pc.shape
    wrows = width // (4 * nz)
    full = lambda a: pl.BlockSpec(a.shape, lambda i, m: (0,) * a.ndim)
    outs = [
        jax.ShapeDtypeStruct((2 * rows, width), F32),
        jax.ShapeDtypeStruct((2 * rows, width), BF),
    ] + [jax.ShapeDtypeStruct((nz, wrows, width + 128), BF)] * 4
    ins = [back, hidden, moe_in, gates, mixture, wo]
    return pl.pallas_call(
        functools.partial(combine_kernel, (nz, experts)),
        grid_spec=pltpu.PrefetchScalarGridSpec(
            num_scalar_prefetch=1,
            grid=(1,),
            in_specs=[full(a) for a in ins] + [full(a) for a in (extras, gains, cols, pc, sc)],
            out_specs=[full(o) for o in outs],
            scratch_shapes=[pltpu.VMEM((width, width + 128), F32)],
        ),
        out_shape=outs,
        compiler_params=PARAMS,
        cost_estimate=pl.CostEstimate(flops=3 << 30, bytes_accessed=10 << 20, transcendentals=0),
        name="combine",
    )(meta, *ins, extras, gains, cols, pc, sc)


def expert_kernel(a_ref, h_ref, up_ref, act_ref, u_ref, back_ref, acc, gg):
    step = pl.program_id(0)
    width = acc.shape[1]

    @pl.when(step == 0)
    def _():
        acc[...] = jnp.zeros_like(acc)
        gg[...] = jnp.zeros_like(gg)

    rows = acc.shape[0]
    block = 256

    def part(i, carry):
        at = pl.ds(pl.multiple_of(i * block, block), block)
        v = dot(a_ref[at, :width], up_ref[0])
        h = h_ref[at, :].astype(F32)
        square = v * v
        t = jnp.tanh(v * (0.7978845608028654 + 0.7978845608028654 * 0.044715 * square))
        half = 0.5 * (1.0 + t)
        act = v * half
        slope = half + 0.5 * v * (1.0 - t * t) * (0.7978845608028654 + 3 * 0.7978845608028654 * 0.044715 * square)
        act_ref[at, :] = act.astype(BF)
        u = (h * slope).astype(BF)
        u_ref[at, :] = u
        gg[at, :] += jnp.broadcast_to(jnp.sum(act * h, axis=1, keepdims=True), (block, 128))
        acc[at, :] += dot(u, up_ref[0], 1, 1)
        return carry

    lax.fori_loop(0, rows // block, part, 0)

    @pl.when(step == pl.num_programs(0) - 1)
    def _():
        back_ref[:, :width] = acc[...].astype(BF)
        back_ref[:, width:] = lane_pair(gg[:, 0:1], 0)


def expert_pass(arrived, h, up):
    rows = arrived.shape[0]
    width, hidden = up.shape[1:]
    tile = 512
    const = lambda j: (0, 0)
    return pl.pallas_call(
        expert_kernel,
        grid=(hidden // tile,),
        in_specs=[
            pl.BlockSpec(arrived.shape, const),
            pl.BlockSpec((rows, tile), lambda j: (0, j)),
            pl.BlockSpec((1, width, tile), lambda j: (0, 0, j)),
        ],
        out_specs=[
            pl.BlockSpec((rows, tile), lambda j: (0, j)),
            pl.BlockSpec((rows, tile), lambda j: (0, j)),
            pl.BlockSpec((rows, width + 128), const),
        ],
        scratch_shapes=[pltpu.VMEM((rows, width), F32), pltpu.VMEM((rows, 128), F32)],
        out_shape=[
            jax.ShapeDtypeStruct((rows, hidden), BF),
            jax.ShapeDtypeStruct((rows, hidden), BF),
            jax.ShapeDtypeStruct((rows, width + 128), BF),
        ],
        compiler_params=PARAMS,
        cost_estimate=pl.CostEstimate(flops=4 * rows * width * hidden, bytes_accessed=30 << 20, transcendentals=0),
        name="experts",
    )(arrived, h, up)


def rows_back_kernel(dims, meta, dk_ref, dv_ref, w_ref, keep0, keep1, send0, send1, scr):
    nz, nc, rows, width = dims
    scr[...] = dot(dk_ref[...], w_ref[:, width : 2 * width], 1, 1) + dot(dv_ref[...], w_ref[:, 2 * width : 3 * width], 1, 1)
    n = 0
    for i, out in enumerate((keep0, keep1, send0, send1)):
        for k in range(nz):
            out[k] = scr[pl.ds(pl.multiple_of(meta[n] * rows, rows), rows), :].astype(BF)
            n += 1
        at = nc * nz * rows + meta[nc * nz + i] * rows
        out[nz] = scr[pl.ds(pl.multiple_of(at, rows), rows), :].astype(BF)


def rows_back(meta, dk, dv, project_full, nz, nc, rows):
    total, width = dk.shape
    tile = 256
    full = lambda a: pl.BlockSpec(a.shape, lambda i, m: (0, 0))
    out = jax.ShapeDtypeStruct((nz + 1, rows, width), BF)
    return pl.pallas_call(
        functools.partial(rows_back_kernel, (nz, nc, rows, width)),
        grid_spec=pltpu.PrefetchScalarGridSpec(
            num_scalar_prefetch=1,
            grid=(width // tile,),
            in_specs=[full(dk), full(dv), pl.BlockSpec((tile, project_full.shape[1]), lambda i, m: (i, 0))],
            out_specs=[pl.BlockSpec((nz + 1, rows, tile), lambda i, m: (0, 0, i))] * 4,
            scratch_shapes=[pltpu.VMEM((total, tile), F32)],
        ),
        out_shape=[out] * 4,
        compiler_params=PARAMS,
        cost_estimate=pl.CostEstimate(flops=4 * total * width * width, bytes_accessed=16 << 20, transcendentals=0),
        name="rows_back",
    )(meta, dk, dv, project_full)


def weights_back_kernel(dims, meta, normed_ref, dq_ref, dk_ref, dv_ref, table_ref, keep0, keep1, send0, send1, scr):
    nz, nc, rows = dims
    width = normed_ref.shape[1]
    wrows = width // (nc * nz)
    step = pl.program_id(0)

    @pl.when(step == 0)
    def _():
        own = pl.multiple_of(meta[nc * nz] * rows, rows)
        own_s = pl.multiple_of(nc * nz * rows + meta[nc * nz + 1] * rows, rows)
        mine = jnp.concatenate([normed_ref[pl.ds(own, rows), :], normed_ref[pl.ds(own_s, rows), :]], axis=0)
        scr[...] = dot(mine, dq_ref[...], 0, 0)
        nb, heads = table_ref.shape
        tb = nb // (nc * nz)
        low = table_ref[...].astype(BF)
        spot = lax.broadcasted_iota(jnp.int32, (16, nb), 0)
        n = 0
        for out in (keep0, keep1, send0, send1):
            for k in range(nz):
                base = meta[n] * tb
                pick = (lax.broadcasted_iota(jnp.int32, (16, nb), 1) == spot + base) & (spot < tb)
                out[k, 3 * wrows :, :] = jnp.zeros((16, width), BF)
                out[k, 3 * wrows :, :heads] = dot(pick.astype(BF), low).astype(BF)
                n += 1

    @pl.when(step == 1)
    def _():
        scr[...] = dot(normed_ref[...], dk_ref[...], 0, 0)

    @pl.when(step == 2)
    def _():
        scr[...] = dot(normed_ref[...], dv_ref[...], 0, 0)

    for part in range(3):

        @pl.when(step == part)
        def _(part=part):
            n = 0
            for out in (keep0, keep1, send0, send1):
                for k in range(nz):
                    chunk = scr[pl.ds(pl.multiple_of(meta[n] * wrows, 8), wrows), :]
                    out[k, part * wrows : (part + 1) * wrows, :] = chunk.astype(BF)
                    n += 1


def weights_back(meta, normed, dq, dk, dv, table, nz, nc, rows):
    total, width = normed.shape
    wrows = width // (nc * nz)
    full = lambda a: pl.BlockSpec(a.shape, lambda i, m: (0,) * a.ndim)
    out = jax.ShapeDtypeStruct((nz, 3 * wrows + 16, width), BF)
    return pl.pallas_call(
        functools.partial(weights_back_kernel, (nz, nc, rows)),
        grid_spec=pltpu.PrefetchScalarGridSpec(
            num_scalar_prefetch=1,
            grid=(3,),
            in_specs=[full(a) for a in (normed, dq, dk, dv, table)],
            out_specs=[full(out)] * 4,
            scratch_shapes=[pltpu.VMEM((width, width), F32)],
        ),
        out_shape=[out] * 4,
        compiler_params=PARAMS,
        cost_estimate=pl.CostEstimate(flops=4 * total * width * width, bytes_accessed=18 << 20, transcendentals=0),
        name="weights_back",
    )(meta, normed, dq, dk, dv, table)


def slots_of(routes, experts, capacity, base):
    hot = [(routes[:, s : s + 1] == jnp.arange(experts, dtype=jnp.int32)[None, :]) for s in range(2)]
    count = (hot[0] | hot[1]).astype(BF)
    n = routes.shape[0]
    before = jnp.arange(n, dtype=jnp.int32)
    tri = (before[:, None] > before[None, :]).astype(BF)
    rank = dot(tri, count)
    return jnp.stack([jnp.sum(jnp.where(h, rank, 0.0), axis=1) for h in hot], axis=1).astype(jnp.int32) + (
        routes * capacity + base
    )


def body(
    prompt_rows,
    suffix_rows,
    prompt_cotangent,
    suffix_cotangent,
    project_weight,
    output_weight,
    router_weight,
    first_gain,
    second_gain,
    bias_table,
    expert_up,
    expert_down,
    prompt_routes,
    suffix_routes,
    suffix_prompt,
    bucket_index,
):
    rows, width = prompt_rows.shape
    tbrows, heads = bias_table.shape
    experts = router_weight.shape[1]
    topk = prompt_routes.shape[1]
    nc, nz, ndp = (lax.axis_size(a) for a in ("context", "expert", "dp"))
    group = nc * nz
    c, z, d = (lax.axis_index(a) for a in ("context", "expert", "dp"))
    owner = c * nz + z
    plen = rows * group // NPROMPT
    slen = rows * nc
    half_capacity = 2 * topk * rows // experts
    capacity = 2 * half_capacity
    slots = experts * capacity
    wrows = width // group
    nb = tbrows * group
    lanes = 128
    suffix_low = suffix_rows.reshape(rows, width)
    suffix_cot = suffix_cotangent.reshape(rows, width)

    ck = jnp.arange(nc, dtype=jnp.int32)
    zk = jnp.arange(nz, dtype=jnp.int32)
    source_c = c ^ ck
    source = (source_c[:, None] * nz + (z + nz - zk[None, :]) % nz).reshape(-1)
    target_c = c ^ jnp.array([core + x for core in (0, context_bits()[1]) for x in (0, context_bits()[0])], jnp.int32)
    target = (target_c[:, None] * nz + (z + zk[None, :]) % nz).reshape(-1)
    gather_meta = jnp.concatenate([source, source_c, owner[None], c[None]]).astype(jnp.int32)
    target_meta = jnp.concatenate([target, target_c]).astype(jnp.int32)
    grads_meta = jnp.concatenate([target, owner[None], c[None]]).astype(jnp.int32)

    extra = jnp.concatenate(
        [
            router_weight,
            first_gain[:, None],
            second_gain[:, None],
            jnp.pad(bias_table, ((0, wrows - tbrows), (0, 0))),
        ],
        axis=1,
    )
    extra = jnp.pad(extra, ((0, 0), (0, lanes - extra.shape[1])))
    extra = jnp.concatenate([extra[8 * i : 8 * i + 8] for i in range(wrows // 8)], axis=1)
    extra = jnp.pad(extra, ((0, 0), (0, width - extra.shape[1])))
    keys = [(i, j) for i in range(nc) for j in range(nz)]
    packed = jnp.concatenate(
        [prompt_rows] + [project_weight[:, i * width : (i + 1) * width] for i in range(3)] + [extra], axis=0
    )
    pieces = gather_group(packed)
    s_pieces = gather_context({(0,): suffix_low})
    o_pieces = gather_group(output_weight)

    suffix_route_rows = suffix_routes.reshape(rows, topk)
    routes = jnp.concatenate([prompt_routes, suffix_route_rows], axis=0)
    flat_slots = jnp.concatenate(
        [
            slots_of(prompt_routes, experts, capacity, 0),
            slots_of(suffix_route_rows, experts, capacity, half_capacity),
        ],
        axis=0,
    )
    slot_ids = jnp.arange(slots, dtype=jnp.int32)[None, :]
    hots = [(flat_slots[:, i : i + 1] == slot_ids).astype(BF) for i in range(topk)]
    cols = jnp.pad(jnp.concatenate([flat_slots, routes], axis=1), ((0, 0), (0, lanes - 2 * topk)))
    slot_rows = jnp.pad(flat_slots.T, ((0, 8 - topk), (0, 0)))
    cot_low = jnp.concatenate([prompt_cotangent, suffix_cot], axis=0)
    cot_sent = dot(hots[0] + hots[1], cot_low, 0, 0).astype(BF)
    cot_arrived = across(cot_sent.reshape(group, capacity, width)).reshape(slots, width)

    q, kv, normed, project_full, extras, gains = project(
        gather_meta, [pieces[k] for k in keys], [s_pieces[(i,)] for i in range(nc)], group, nc, experts
    )

    own_prompt = owner * rows // plen
    first_p = owner * rows - own_prompt * plen
    first_s = plen + c * rows
    dist = bucket_index.shape[0]
    ladder = jnp.concatenate(
        [
            jnp.zeros((rows,), jnp.int32),
            jnp.flip(bucket_index),
            jnp.full((max(plen, slen) + rows,), -1, jnp.int32),
        ]
    )
    bp = lax.dynamic_slice_in_dim(ladder, dist - 1 - first_p, plen + rows)[None, :]
    bs = lax.dynamic_slice_in_dim(ladder, dist - 1 - first_s, plen + slen + rows)[None, :]
    places = jnp.stack([own_prompt, suffix_prompt[0], jnp.int32(NPROMPT * plen // slen)]).astype(jnp.int32)
    mixture, pp, ps = attend((experts, nb, tbrows, wrows), places, q, kv, extras, bp, bs, plen, slen)
    hidden, moe_in, gates, sent, output_full = post(
        gather_meta, prompt_rows, suffix_low, mixture, extras, gains, cols, slot_rows,
        [o_pieces[k] for k in keys], group, experts, slots,
    )
    arrived = across(sent.reshape(group, capacity, width + lanes)).reshape(slots, width + lanes)

    h = dot(cot_arrived, expert_down[0], 1, 1).astype(BF)
    act, u, back = expert_pass(arrived, h, expert_up)
    back_in = across(back.reshape(group, capacity, width + lanes)).reshape(slots, width + lanes)
    gate_in = jnp.sum(arrived[:, width:].astype(F32), axis=1, keepdims=True)
    tokens = arrived[:, :width]
    gated_cot = (gate_in * cot_arrived.astype(F32)).astype(BF)
    gated_u = (gate_in * u.astype(F32)).astype(BF)
    produced = dot(act, expert_down[0]).astype(BF)
    returned = across(produced.reshape(group, capacity, width)).reshape(slots, width)

    hidden_units = expert_up.shape[2]
    down_rows, up_rows = hidden_units // ndp, width // ndp

    def down_part(i, a, g):
        return dot(lax.dynamic_slice_in_dim(a, i * down_rows, down_rows, 1), g, 0, 0)

    def up_part(i, a, g):
        return dot(lax.dynamic_slice_in_dim(a, i * up_rows, up_rows, 1), g, 0, 0)

    down_got = [shift(down_part((d + k) % ndp, act, gated_cot).astype(BF), "dp", k) for k in range(1, ndp)]
    up_got = [shift(up_part((d + k) % ndp, tokens, gated_u).astype(BF), "dp", k) for k in range(1, ndp)]

    hidden_grad, mixture_grad, *early = combine(
        target_meta, back_in, hidden, moe_in, gates, mixture, output_full, extras, gains, cols,
        prompt_cotangent, suffix_cot, nz, experts,
    )
    dq, dk, dv, table_grad = attend_back(places, q, mixture_grad, kv, pp, ps, bp, bs, plen, slen, nb)
    early = reduce_rows(*early, nz)[0]
    early = reduce_dp(early)
    chunks = rows_back(target_meta, dk, dv, project_full, nz, nc, rows)
    prompt_part, suffix_part = reduce_rows(*chunks, nz)
    late = reduce_rows(*weights_back(grads_meta, normed, dq, dk, dv, table_grad, nz, nc, rows), nz)[0]
    late = reduce_dp(late)

    down_own = down_part(d, act, gated_cot)
    up_own = up_part(d, tokens, gated_u)
    down_own, up_own = lax.optimization_barrier((down_own, up_own))
    down_shard = (down_own + sum(g.astype(F32) for g in down_got))[None]
    up_shard = (up_own + sum(g.astype(F32) for g in up_got))[None]
    result = hidden + gates[:, 0:1] * dot(hots[0], returned) + gates[:, 1:2] * dot(hots[1], returned)

    project_shard = late[: 3 * wrows].reshape(3, wrows, width).transpose(1, 0, 2).reshape(wrows, 3 * width)
    first_shard = jnp.sum(project_shard * project_weight.astype(F32), axis=1) / first_gain.astype(F32)
    normed_total = jnp.concatenate([prompt_part, suffix_part[0]], axis=0) + dot(dq, project_full[:, :width], 1, 1)
    inputs = jnp.concatenate([prompt_rows, suffix_low], axis=0).astype(F32)
    scale = lax.rsqrt(jnp.mean(inputs * inputs, axis=-1, keepdims=True) + EPS)
    hat = inputs * scale
    gy = normed_total * gains[0:1, :]
    input_grad = hidden_grad + scale * (gy - hat * jnp.mean(gy * hat, axis=-1, keepdims=True))
    return (
        result[:rows].astype(BF),
        result[rows:].astype(BF).reshape(suffix_rows.shape),
        input_grad[:rows],
        input_grad[rows:].reshape(suffix_rows.shape),
        project_shard,
        early[:, :width],
        early[:, width : width + experts],
        first_shard,
        early[:, width + experts],
        late[3 * wrows : 3 * wrows + tbrows, :heads],
        up_shard,
        down_shard,
    )


def solution(mesh):
    return jax.shard_map(
        body,
        mesh=mesh,
        in_specs=(
            P(("dp", "context", "expert"), None),
            P("context", ("dp", "expert"), None, None),
            P(("dp", "context", "expert"), None),
            P("context", ("dp", "expert"), None, None),
            P(("context", "expert"), None),
            P(("context", "expert"), None),
            P(("context", "expert"), None),
            P(("context", "expert")),
            P(("context", "expert")),
            P(("context", "expert"), None),
            P(("context", "expert"), None, None),
            P(("context", "expert"), None, None),
            P(("dp", "context", "expert"), None),
            P("context", ("dp", "expert"), None, None),
            P(("dp", "expert")),
            P(),
        ),
        out_specs=(
            P(("dp", "context", "expert"), None),
            P("context", ("dp", "expert"), None, None),
            P(("dp", "context", "expert"), None),
            P("context", ("dp", "expert"), None, None),
            P(("context", "expert"), None),
            P(("context", "expert"), None),
            P(("context", "expert"), None),
            P(("context", "expert")),
            P(("context", "expert")),
            P(("context", "expert"), None),
            P(("context", "expert"), "dp", None),
            P(("context", "expert"), "dp", None),
        ),
        check_vma=False,
    )
```
